32 devices in a mesh: dp: 4 (over y, core), ctx: 8 (over z, x).
Axes of the slice: x: 2, y: 2, z: 4, core: 2. Of those that a mesh axis runs over, the one named last changes fastest.
Arguments:
- queries: bfloat16 [4, 8192, 1024], P('dp', 'ctx'), may hold values from -160 to 160
- keys: bfloat16 [4, 8192, 1024], P('dp', 'ctx'), may hold values from -14 to 14
- values: bfloat16 [4, 8192, 1024], P('dp', 'ctx'), may hold values from -4.5 to 4.5
- cotangent: bfloat16 [4, 8192, 1024], P('dp', 'ctx'), may hold values from -6 to 6
- gain: float32 [1024], replicated, may hold values from 0.1 to 1.9
Outputs:
- attended: bfloat16 [4, 8192, 1024], P('dp', 'ctx')
- grad_queries: bfloat16 [4, 8192, 1024], P('dp', 'ctx')
- grad_keys: bfloat16 [4, 8192, 1024], P('dp', 'ctx')
- grad_values: bfloat16 [4, 8192, 1024], P('dp', 'ctx')
- gain_grad: float32 [1024], replicated
The draws below stay inside these ranges and needn't reach their ends.
All inputs are finite; a program needn't handle non-finite values.
Results may differ from the reference program's by a relative error of at most 0.019.
The reference program's roundings to bfloat16 on the way count: a program that leaves them out, or rounds other values in their place, can miss the bound.
Values may be sent and summed in bfloat16 or wider, within the bound.
No kernel may reach another device: no remote copies, remote signals or barrier semaphores. Data moves between devices by JAX's collectives and lax.ppermute only.
A program may use at most 192 MiB of HBM per device.

```python
import jax
import jax.numpy as jnp
from jax import lax

H = 8
HD = 128
BLOCK = 128
STRIDE = 1024
SUMMARY = 8
D = 1024
SEQ = 8192
BATCH = 4


def shared_keys(key):
    base = jnp.clip(jax.random.normal(jax.random.fold_in(key, 11), (BATCH, SEQ, H * HD), jnp.float32), -4.5, 4.5)
    return base


def draw_keys(key, part):
    return shared_keys(key).astype(jnp.bfloat16)


def draw_queries(key, part):
    noise = jnp.clip(jax.random.normal(jax.random.fold_in(key, 13), (BATCH, SEQ, H * HD), jnp.float32), -4.5, 4.5) * 2.0
    return noise.astype(jnp.bfloat16)


def levels(stream_key, shape, shards, smallest, top_value):
    factor_of = 1.0
    for dim, parts in shards:
        steps = jax.random.uniform(jax.random.fold_in(jax.random.fold_in(stream_key, 6), dim), (parts,), jnp.float32, smallest / len(shards), top_value / len(shards))
        factor_of = factor_of * jnp.repeat(jnp.exp(steps), shape[dim] // parts).reshape((-1,) + (1,) * (len(shape) - 1 - dim))
    return factor_of


def gaussian(own_key, shape, deviation, most, split=(), held_as=jnp.bfloat16):
    factor_of = levels(own_key, shape, split, -0.22, 0.18) if split else 1.0
    drawn = jax.random.normal(own_key, shape, jnp.float32) * deviation * factor_of
    return jnp.minimum(jnp.maximum(drawn, -most), most).astype(held_as)


def setup_inputs(seed: int = 0) -> dict:
    key_list = jax.random.split(jax.random.key(seed), 6)
    queries = draw_queries(jax.random.fold_in(key_list[5], 71), 0)
    keys = draw_keys(jax.random.fold_in(key_list[5], 71), 0)
    values = gaussian(key_list[2], (BATCH, SEQ, D), 1.0, 4.5, ((0, 4), (1, 8)))
    cotangent = gaussian(key_list[3], (BATCH, SEQ, D), 1.0, 6.0, ((0, 4), (1, 8)))
    gain = jnp.clip(1.0 + 0.18 * jax.random.normal(key_list[4], (D,), jnp.float32), 0.1, 1.9)
    return {"queries": queries, "keys": keys, "values": values, "cotangent": cotangent, "gain": gain}


NEG = -1e30


def to_rows(block_array):
    blocks, heads, width = block_array.shape
    return block_array.transpose(1, 0, 2).reshape(heads, blocks * width)


def to_blocks(row_array, blocks):
    heads, length = row_array.shape
    return row_array.reshape(heads, blocks, length // blocks).transpose(1, 0, 2)


def sequence_pass(queries, keys, values, cotangent, gain):
    f32 = jnp.float32
    bf16 = jnp.bfloat16
    length = queries.shape[0]
    blocks = length // BLOCK
    segs = length // STRIDE
    total_sums = segs * SUMMARY
    scale = HD ** -0.5
    scaled = (queries.astype(f32) * gain).astype(bf16)
    padding = jnp.zeros((BLOCK, H * HD), bf16)
    ext_keys = jnp.concatenate([padding, keys], 0).reshape(blocks + 1, BLOCK, H, HD)
    ext_values = jnp.concatenate([padding, values], 0).reshape(blocks + 1, BLOCK, H, HD)
    band_keys = jnp.concatenate([ext_keys[:-1], ext_keys[1:]], 1)
    band_values = jnp.concatenate([ext_values[:-1], ext_values[1:]], 1)
    query_blocks = scaled.reshape(blocks, BLOCK, H, HD)
    scaled_rows = scaled.reshape(length, H, HD)
    sum_keys = keys.reshape(segs, STRIDE, H * HD)[:, STRIDE - SUMMARY:].reshape(total_sums, H, HD)
    sum_values = values.reshape(segs, STRIDE, H * HD)[:, STRIDE - SUMMARY:].reshape(total_sums, H, HD)
    query_index = jnp.arange(BLOCK)[:, None]
    key_index = jnp.arange(2 * BLOCK)[None, :]
    band = (key_index > query_index) & (key_index <= query_index + BLOCK)
    later_block = jnp.arange(blocks)[:, None, None] > 0
    band_mask = (band[None] & (later_block | (key_index >= BLOCK)[None]))[:, None]
    slot = jnp.arange(total_sums)
    sum_pos = (slot // SUMMARY) * STRIDE + STRIDE - SUMMARY + slot % SUMMARY
    query_pos = jnp.arange(length)
    sum_mask = (query_pos[:, None] - sum_pos[None, :] >= BLOCK)[None]
    band_scores = jnp.einsum("nqhd,nkhd->nhqk", query_blocks.astype(f32), band_keys.astype(f32)) * scale
    band_scores = jnp.where(band_mask, band_scores, NEG)
    sum_scores = jnp.einsum("qhd,shd->hqs", scaled_rows.astype(f32), sum_keys.astype(f32)) * scale
    sum_scores = jnp.where(sum_mask, sum_scores, NEG)
    top = jnp.maximum(to_rows(jnp.max(band_scores, -1)), jnp.max(sum_scores, -1))
    band_exp = jnp.where(band_mask, jnp.exp(band_scores - to_blocks(top, blocks)[..., None]), 0.0)
    sum_exp = jnp.where(sum_mask, jnp.exp(sum_scores - top[..., None]), 0.0)
    total = to_rows(jnp.sum(band_exp, -1)) + jnp.sum(sum_exp, -1)
    band_prob = band_exp / to_blocks(total, blocks)[..., None]
    sum_prob = sum_exp / total[..., None]
    band_prob_b = band_prob.astype(bf16)
    sum_prob_b = sum_prob.astype(bf16)
    mixed = jnp.einsum("nhqk,nkhd->nqhd", band_prob_b.astype(f32), band_values.astype(f32)).reshape(length, H, HD)
    mixed = mixed + jnp.einsum("hqs,shd->qhd", sum_prob_b.astype(f32), sum_values.astype(f32))
    attended = mixed.reshape(length, H * HD).astype(bf16)
    grad_rows = cotangent.reshape(length, H, HD).astype(f32)
    grad_blocks = grad_rows.reshape(blocks, BLOCK, H, HD)
    delta = jnp.sum(grad_rows * attended.reshape(length, H, HD).astype(f32), -1).T
    band_dprob = jnp.einsum("nqhd,nkhd->nhqk", grad_blocks, band_values.astype(f32))
    sum_dprob = jnp.einsum("qhd,shd->hqs", grad_rows, sum_values.astype(f32))
    band_ds = (band_prob * (band_dprob - to_blocks(delta, blocks)[..., None]) * scale).astype(bf16)
    sum_ds = (sum_prob * (sum_dprob - delta[..., None]) * scale).astype(bf16)
    band_dv = jnp.einsum("nhqk,nqhd->nkhd", band_prob_b.astype(f32), grad_blocks)
    band_dk = jnp.einsum("nhqk,nqhd->nkhd", band_ds.astype(f32), query_blocks.astype(f32))

    def fold_band(pairs):
        later = jnp.concatenate([pairs[1:, :BLOCK], jnp.zeros((1, BLOCK, H, HD), f32)], 0)
        return (pairs[:, BLOCK:] + later).reshape(segs, STRIDE, H * HD)

    sum_dv = jnp.einsum("hqs,qhd->shd", sum_prob_b.astype(f32), grad_rows).reshape(segs, SUMMARY, H * HD)
    sum_dk = jnp.einsum("hqs,qhd->shd", sum_ds.astype(f32), scaled_rows.astype(f32)).reshape(segs, SUMMARY, H * HD)
    grad_values = fold_band(band_dv).at[:, STRIDE - SUMMARY:].add(sum_dv).reshape(length, H * HD).astype(bf16)
    grad_keys = fold_band(band_dk).at[:, STRIDE - SUMMARY:].add(sum_dk).reshape(length, H * HD).astype(bf16)
    grad_scaled = jnp.einsum("nhqk,nkhd->nqhd", band_ds.astype(f32), band_keys.astype(f32)).reshape(length, H, HD)
    grad_scaled = grad_scaled + jnp.einsum("hqs,shd->qhd", sum_ds.astype(f32), sum_keys.astype(f32))
    grad_scaled = grad_scaled.reshape(length, H * HD)
    grad_queries = (grad_scaled * gain).astype(bf16)
    gain_part = jnp.sum(grad_scaled * queries.astype(f32), 0)
    return attended, grad_queries, grad_keys, grad_values, gain_part


def reference(queries, keys, values, cotangent, gain):
    results = lax.map(lambda items: sequence_pass(items[0], items[1], items[2], items[3], gain), (queries, keys, values, cotangent))
    attended, grad_queries, grad_keys, grad_values, gain_parts = results
    gain_grad = jnp.sum(gain_parts, 0) * (BATCH * SEQ) ** -0.5
    return attended, grad_queries, grad_keys, grad_values, gain_grad
```

```python
import functools

import jax
import jax.numpy as jnp
from jax import lax
from jax.experimental import pallas as pl
from jax.experimental.pallas import tpu as pltpu
from jax.sharding import PartitionSpec as P


H = 8
HD = 128
BLOCK = 128
STRIDE = 1024
SUMMARY = 8
NEG = -1e30
SCALE = HD**-0.5
EXP2_SCALE = SCALE * 1.4426950408889634

f32 = jnp.float32
bf16 = jnp.bfloat16


def from_behind(value, axis, steps):
    count = lax.axis_size(axis)
    first, last = (max(0, -steps), min(count, count - steps))
    return lax.ppermute(value, axis, [(source, source + steps) for source in range(first, last)])


def nt(a, b):
    return lax.dot_general(a, b, (((1,), (1,)), ((), ())), preferred_element_type=f32)


def nn(a, b):
    return lax.dot_general(a, b, (((1,), (0,)), ((), ())), preferred_element_type=f32)


def unpack_sums(ref):
    wide = ref[...].astype(f32)
    sources, both, width = wide.shape
    own = both // 2
    keys = wide[:, :own].reshape(sources * own, width)
    values = wide[:, own:].reshape(sources * own, width)
    return keys.astype(bf16), values.astype(bf16)


def sum_bias(total_sums, segment, first_block):
    slot = lax.broadcasted_iota(jnp.int32, (total_sums, BLOCK), 0)
    query = lax.broadcasted_iota(jnp.int32, (total_sums, BLOCK), 1)
    position = slot // SUMMARY * STRIDE + STRIDE - SUMMARY + slot % SUMMARY
    start = segment * STRIDE + (0 if first_block else BLOCK)
    return jnp.where(start + query - position >= BLOCK, 0.0, NEG).astype(f32)


def block_probs(keys2, values2, sum_keys, sum_values, scaled, grads, bias, tri, no_prev):
    s = nt(keys2, scaled)
    ss = nt(sum_keys, scaled) + bias
    dp = nt(values2, grads)
    dps = nt(sum_values, grads)
    prev = s[:BLOCK]
    if no_prev is not None:
        prev = jnp.where(no_prev, NEG, prev)
    sm = jnp.where(tri, s[BLOCK:], prev)
    dpm = jnp.where(tri, dp[BLOCK:], dp[:BLOCK])
    top = jnp.maximum(jnp.max(sm, 0, keepdims=True), jnp.max(ss, 0, keepdims=True))
    e = jnp.exp2((sm - top) * EXP2_SCALE)
    es = jnp.exp2((ss - top) * EXP2_SCALE)
    total = jnp.sum(e, 0, keepdims=True) + jnp.sum(es, 0, keepdims=True)
    inv = 1.0 / total
    p = e * inv
    ps = es * inv
    delta = jnp.sum(p * dpm, 0, keepdims=True) + jnp.sum(ps * dps, 0, keepdims=True)
    pb = p.astype(bf16)
    psb = ps.astype(bf16)
    ds = p * (dpm - delta) * SCALE
    dss = ps * (dps - delta) * SCALE
    return pb, psb, ds.astype(bf16), dss.astype(bf16)


def rim_kernel(segs, rank_ref, q, k, v, g, rim, sums, gain, out):
    rank = rank_ref[0]
    total_sums = sums.shape[0] * (sums.shape[1] // 2)
    bias = sum_bias(total_sums, rank * segs, True)
    key_at = lax.broadcasted_iota(jnp.int32, (BLOCK, BLOCK), 0)
    query_at = lax.broadcasted_iota(jnp.int32, (BLOCK, BLOCK), 1)
    tri = key_at <= query_at
    zero = jnp.zeros((BLOCK, BLOCK), bf16)
    for h in range(H):
        cols = slice(h * HD, (h + 1) * HD)
        sk, sv = unpack_sums(sums.at[:, :, cols])
        scaled = (q[:, cols].astype(f32) * gain[:, cols]).astype(bf16)
        grads = g[:, cols]
        keys2 = jnp.concatenate([rim[:BLOCK, cols], k[:, cols]], 0)
        values2 = jnp.concatenate([rim[BLOCK:, cols], v[:, cols]], 0)
        pb, _, ds, _ = block_probs(keys2, values2, sk, sv, scaled, grads, bias, tri, rank == 0)
        out[:BLOCK, cols] = nn(jnp.where(tri, zero, ds), scaled).astype(bf16)
        out[BLOCK:, cols] = nn(jnp.where(tri, zero, pb), grads).astype(bf16)


def main_kernel(
    segs, rank_ref, q, k, v, g, rim, sums, gain,
    att, gq, gk, gv, tails, sum_grads, gain_part,
    kx, vx, sc, bias_ref,
):
    rank = rank_ref[0]
    sources, both, _ = sums.shape
    total_sums = sources * both // 2
    blocks = q.shape[0] // BLOCK
    per_seg = STRIDE // BLOCK

    @pl.when(pl.program_id(0) == 0)
    def _():
        for seg in range(segs):
            bias_ref[2 * seg] = sum_bias(total_sums, rank * segs + seg, True)
            bias_ref[2 * seg + 1] = sum_bias(total_sums, rank * segs + seg, False)

    key_at = lax.broadcasted_iota(jnp.int32, (BLOCK, BLOCK), 0)
    query_at = lax.broadcasted_iota(jnp.int32, (BLOCK, BLOCK), 1)
    tri = key_at <= query_at
    low = query_at <= key_at
    zero = jnp.zeros((BLOCK, BLOCK), bf16)
    kx[:BLOCK] = rim[:BLOCK]
    kx[BLOCK:] = k[...]
    vx[:BLOCK] = rim[BLOCK:]
    vx[BLOCK:] = v[...]
    gain_row = gain[...]
    sc[...] = (q[...].astype(f32) * gain_row).astype(bf16)
    sk, sv = unpack_sums(sums)
    gain_sum = jnp.zeros((1, HD), f32)
    sum_dk = jnp.zeros((total_sums, HD), f32)
    sum_dv = jnp.zeros((total_sums, HD), f32)
    p_own = ds_own = None
    for b in range(blocks):
        rows = slice(b * BLOCK, (b + 1) * BLOCK)
        two = slice(b * BLOCK, (b + 2) * BLOCK)
        back = slice((b - 1) * BLOCK, (b + 1) * BLOCK)
        scaled = sc[rows]
        grads = g[rows]
        bias = bias_ref[2 * (b // per_seg) + (0 if b % per_seg == 0 else 1)]
        pb, psb, ds, dss = block_probs(
            kx[two], vx[two], sk, sv, scaled, grads, bias, tri, rank == 0 if b == 0 else None
        )
        sum_dv = sum_dv + nn(psb, grads)
        sum_dk = sum_dk + nn(dss, scaled)
        if b > 0:
            before = slice((b - 1) * BLOCK, b * BLOCK)
            dv = nn(jnp.concatenate([p_own, jnp.where(tri, zero, pb)], 1), g[back])
            dk = nn(jnp.concatenate([ds_own, jnp.where(tri, zero, ds)], 1), sc[back])
            if b % per_seg == 0:
                at = (b // per_seg - 1) * 2 * BLOCK
                tails[at : at + BLOCK] = dk
                tails[at + BLOCK : at + 2 * BLOCK] = dv
            else:
                gk[before] = dk.astype(bf16)
                gv[before] = dv.astype(bf16)
        p_own = jnp.where(tri, pb, zero)
        ds_own = jnp.where(tri, ds, zero)
        pt = pb.T
        dst = ds.T
        pcat = jnp.concatenate([jnp.where(low, zero, pt), jnp.where(low, pt, zero)], 1)
        o = nn(pcat, vx[two]) + nn(psb.T, sv)
        att[rows] = o.astype(bf16)
        dcat = jnp.concatenate([jnp.where(low, zero, dst), jnp.where(low, dst, zero)], 1)
        dq = nn(dcat, kx[two]) + nn(dss.T, sk)
        gq[rows] = (dq * gain_row).astype(bf16)
        gain_sum = gain_sum + jnp.sum(dq * q[rows].astype(f32), 0, keepdims=True)
    at = (segs - 1) * 2 * BLOCK
    tails[at : at + BLOCK] = nn(ds_own, scaled)
    tails[at + BLOCK : at + 2 * BLOCK] = nn(p_own, grads)
    own = both // 2
    sum_grads[...] = jnp.concatenate(
        [sum_dk.reshape(sources, own, HD), sum_dv.reshape(sources, own, HD)], 1
    ).astype(bf16)
    gain_part[...] = gain_sum


def finish_kernel(segs, gk_in, gv_in, tails, rim, sums, gk, gv):
    del gk_in, gv_in
    seg = pl.program_id(0)
    last = seg == segs - 1
    dk = tails[:BLOCK]
    dv = tails[BLOCK:]
    rim_dk = rim[:BLOCK].astype(f32)
    rim_dv = rim[BLOCK:].astype(f32)
    if segs > 1:
        rim_dk = jnp.where(last, rim_dk, 0.0)
        rim_dv = jnp.where(last, rim_dv, 0.0)
    total = jnp.sum(sums[...].astype(f32), 0)
    own = segs * SUMMARY
    body = BLOCK - SUMMARY
    dk = dk + rim_dk
    dv = dv + rim_dv
    sk = total[:SUMMARY]
    sv = total[own : own + SUMMARY]
    for other in range(1, segs):
        at = other * SUMMARY
        sk = jnp.where(seg == other, total[at : at + SUMMARY], sk)
        sv = jnp.where(seg == other, total[own + at : own + at + SUMMARY], sv)
    gk[...] = jnp.concatenate([dk[:body], dk[body:] + sk], 0).astype(bf16)
    gv[...] = jnp.concatenate([dv[:body], dv[body:] + sv], 0).astype(bf16)


def per_device(queries, keys, values, cotangent, gain):
    batch, length, width = queries.shape
    segs = length // STRIDE
    own = segs * SUMMARY
    n = lax.axis_size("ctx")
    rank = lax.axis_index("ctx")
    total_sums = n * own
    q, k, v, g = (a.reshape(length, width) for a in (queries, keys, values, cotangent))
    gain_row = gain.reshape(1, width)
    rank1 = rank.reshape(1).astype(jnp.int32)

    rim = from_behind(
        jnp.concatenate([k[length - BLOCK :], v[length - BLOCK :]], 0), "ctx", 1
    )
    own_keys = k.reshape(segs, STRIDE, width)[:, STRIDE - SUMMARY :].reshape(own, width)
    own_values = v.reshape(segs, STRIDE, width)[:, STRIDE - SUMMARY :].reshape(own, width)
    own_both = jnp.concatenate([own_keys, own_values], 0)
    sums = lax.all_to_all(jnp.broadcast_to(own_both[None], (n, 2 * own, width)), "ctx", 0, 0)

    smem = pl.BlockSpec(memory_space=pltpu.SMEM)
    first = pl.BlockSpec((BLOCK, width), lambda i: (0, 0))
    whole = lambda *shape: pl.BlockSpec(shape, lambda i: (0,) * len(shape))
    rim_grads = pl.pallas_call(
        functools.partial(rim_kernel, segs),
        grid=(1,),
        in_specs=[smem, first, first, first, first, whole(2 * BLOCK, width),
                  whole(n, 2 * own, width), whole(1, width)],
        out_specs=whole(2 * BLOCK, width),
        out_shape=jax.ShapeDtypeStruct((2 * BLOCK, width), bf16),
        cost_estimate=pl.CostEstimate(flops=500_000_000, bytes_accessed=3 << 20, transcendentals=0),
        name="rim_grads",
    )(rank1, q, k, v, g, rim, sums, gain_row)
    received = from_behind(rim_grads, "ctx", -1)
    q, rim_grads = lax.optimization_barrier((q, rim_grads))

    col = lambda rows: pl.BlockSpec((rows, HD), lambda h: (0, h))
    col3 = pl.BlockSpec((n, 2 * own, HD), lambda h: (0, 0, h))
    big = jax.ShapeDtypeStruct((length, width), bf16)
    main = pl.pallas_call(
        functools.partial(main_kernel, segs),
        grid=(H,),
        in_specs=[smem, col(length), col(length), col(length), col(length), col(2 * BLOCK),
                  col3, col(1)],
        out_specs=[col(length)] * 4 + [col(segs * 2 * BLOCK), col3, col(1)],
        out_shape=[big] * 4 + [
            jax.ShapeDtypeStruct((segs * 2 * BLOCK, width), f32),
            jax.ShapeDtypeStruct((n, 2 * own, width), bf16),
            jax.ShapeDtypeStruct((1, width), f32),
        ],
        scratch_shapes=[
            pltpu.VMEM((length + BLOCK, HD), bf16),
            pltpu.VMEM((length + BLOCK, HD), bf16),
            pltpu.VMEM((length, HD), bf16),
            pltpu.VMEM((2 * segs, total_sums, BLOCK), f32),
        ],
        cost_estimate=pl.CostEstimate(
            flops=4_000_000_000, bytes_accessed=18 << 20, transcendentals=2_000_000
        ),
        name="band_and_sums",
    )
    att, gq, gk, gv, tails, sum_grads, gain_part = main(
        rank1, q, k, v, g, rim, sums, gain_row
    )

    gain_dp = lax.psum(gain_part, "dp")
    high = gain_dp.astype(bf16)
    low = (gain_dp - high.astype(f32)).astype(bf16)
    gain_rows = jnp.concatenate([high, low], 0)
    payload = jnp.concatenate(
        [sum_grads, jnp.broadcast_to(gain_rows[None], (n, 2, width))], 1
    )
    got = lax.all_to_all(payload, "ctx", 0, 0)
    token_count = batch * lax.axis_size("dp") * length * n
    gain_grad = jnp.sum(got[:, 2 * own :].astype(f32), (0, 1)) * token_count**-0.5
    got_sums = got[:, : 2 * own]

    per_seg = STRIDE // BLOCK
    tail_spec = pl.BlockSpec((2 * BLOCK, width), lambda s: (s, 0))
    last_block = pl.BlockSpec((BLOCK, width), lambda s: (s * per_seg + per_seg - 1, 0))
    raw = pl.BlockSpec(memory_space=pl.ANY)
    gk, gv = pl.pallas_call(
        functools.partial(finish_kernel, segs),
        grid=(segs,),
        in_specs=[raw, raw, tail_spec, whole(2 * BLOCK, width), whole(n, 2 * own, width)],
        out_specs=[last_block, last_block],
        out_shape=[big, big],
        input_output_aliases={0: 0, 1: 1},
        cost_estimate=pl.CostEstimate(flops=1_000_000, bytes_accessed=3 << 20, transcendentals=0),
        name="finish",
    )(gk, gv, tails, received, got_sums)
    return (
        att.reshape(queries.shape), gq.reshape(queries.shape), gk.reshape(queries.shape),
        gv.reshape(queries.shape), gain_grad,
    )


def solution(mesh):
    spec = P("dp", "ctx", None)
    return jax.shard_map(
        per_device, mesh=mesh, in_specs=(spec,) * 4 + (P(),), out_specs=(spec,) * 4 + (P(),),
        check_vma=False,
    )
```

```python
import functools

import jax
import jax.numpy as jnp
from jax import lax
from jax.experimental import pallas as pl
from jax.experimental.pallas import tpu as pltpu
from jax.sharding import PartitionSpec as P


H = 8
HD = 128
BLOCK = 128
STRIDE = 1024
SUMMARY = 8
NEG = -1e30
SCALE = HD**-0.5
EXP2_SCALE = SCALE * 1.4426950408889634

f32 = jnp.float32
bf16 = jnp.bfloat16


def from_behind(value, axis, steps):
    count = lax.axis_size(axis)
    first, last = (max(0, -steps), min(count, count - steps))
    return lax.ppermute(value, axis, [(source, source + steps) for source in range(first, last)])


def nt(a, b):
    return lax.dot_general(a, b, (((1,), (1,)), ((), ())), preferred_element_type=f32)


def nn(a, b):
    return lax.dot_general(a, b, (((1,), (0,)), ((), ())), preferred_element_type=f32)


def unpack_sums(ref):
    wide = ref[...].astype(f32)
    sources, both, width = wide.shape
    own = both // 2
    keys = wide[:, :own].reshape(sources * own, width)
    values = wide[:, own:].reshape(sources * own, width)
    return keys.astype(bf16), values.astype(bf16)


def sum_bias(total_sums, segment, first_block):
    slot = lax.broadcasted_iota(jnp.int32, (total_sums, BLOCK), 0)
    query = lax.broadcasted_iota(jnp.int32, (total_sums, BLOCK), 1)
    position = slot // SUMMARY * STRIDE + STRIDE - SUMMARY + slot % SUMMARY
    start = segment * STRIDE + (0 if first_block else BLOCK)
    return jnp.where(start + query - position >= BLOCK, 0.0, NEG).astype(f32)


def pipeline(count, first, second, third):
    for step in range(count + 2):
        if step < count:
            first(step)
        if 0 <= step - 2:
            third(step - 2)
        if 0 <= step - 1 < count:
            second(step - 1)


def triangle():
    at = [lax.broadcasted_iota(jnp.int32, (BLOCK, BLOCK), axis) for axis in (0, 1)]
    return at[0] <= at[1], at[1] <= at[0]


def score(slot, s_buf, d_buf, keys2, values2, sum_keys, sum_values, scaled, grads, tri, no_prev):
    s = nt(keys2, scaled)
    prev = s[:BLOCK]
    if no_prev is not None:
        prev = jnp.where(no_prev, NEG, prev)
    s_buf[slot, :BLOCK] = jnp.where(tri, s[BLOCK:], prev)
    s_buf[slot, BLOCK:] = nt(sum_keys, scaled)
    d = nt(values2, grads)
    d_buf[slot, :BLOCK] = jnp.where(tri, d[BLOCK:], d[:BLOCK])
    d_buf[slot, BLOCK:] = nt(sum_values, grads)


def soften(slot, s_buf, d_buf, p_buf, ds_buf, bias):
    sm = s_buf[slot, :BLOCK]
    ss = s_buf[slot, BLOCK:] + bias
    top = jnp.maximum(jnp.max(sm, 0, keepdims=True), jnp.max(ss, 0, keepdims=True))
    e = jnp.exp2((sm - top) * EXP2_SCALE)
    es = jnp.exp2((ss - top) * EXP2_SCALE)
    total = jnp.sum(e, 0, keepdims=True) + jnp.sum(es, 0, keepdims=True)
    inv = 1.0 / total
    p = e * inv
    ps = es * inv
    p_buf[slot, :BLOCK] = p.astype(bf16)
    p_buf[slot, BLOCK:] = ps.astype(bf16)
    dm = d_buf[slot, :BLOCK]
    dsum = d_buf[slot, BLOCK:]
    delta = jnp.sum(p * dm, 0, keepdims=True) + jnp.sum(ps * dsum, 0, keepdims=True)
    ds_buf[slot, :BLOCK] = (p * (dm - delta) * SCALE).astype(bf16)
    ds_buf[slot, BLOCK:] = (ps * (dsum - delta) * SCALE).astype(bf16)


def spread(buf, slot, rhs_by_query, rhs_by_key, rhs_by_sum, tri, low):
    zero = jnp.zeros((BLOCK, BLOCK), bf16)
    m = buf[slot, :BLOCK]
    ms = buf[slot, BLOCK:]
    by_key = nn(
        jnp.concatenate([jnp.where(tri, zero, m), jnp.where(tri, m, zero), ms], 0), rhs_by_query
    )
    mt = m.T
    wide = jnp.concatenate([jnp.where(low, zero, mt), jnp.where(low, mt, zero)], 1)
    by_query = nn(wide, rhs_by_key) + nn(ms.T, rhs_by_sum)
    return by_key, by_query


def rim_kernel(
    segs, rank_ref, q, k, v, g, rim, sums, gain,
    att, gq, out, heads_part, sum_part, gain_part,
    s_buf, d_buf, p_buf, ds_buf, sc, sk, sv,
):
    rank = rank_ref[0]
    sources, both, _ = sums.shape
    own = both // 2
    total_sums = sources * own
    bias = sum_bias(total_sums, rank * segs, True)
    tri, low = triangle()

    def cols(h):
        return slice(h * HD, (h + 1) * HD)

    def first(h):
        at = cols(h)
        slot = h % 3
        sk[slot], sv[slot] = unpack_sums(sums.at[:, :, at])
        sc[slot] = (q[:, at].astype(f32) * gain[:, at]).astype(bf16)
        keys2 = jnp.concatenate([rim[:BLOCK, at], k[:, at]], 0)
        values2 = jnp.concatenate([rim[BLOCK:, at], v[:, at]], 0)
        score(slot, s_buf, d_buf, keys2, values2, sk[slot], sv[slot], sc[slot], g[:, at], tri,
              rank == 0)

    def second(h):
        soften(h % 3, s_buf, d_buf, p_buf, ds_buf, bias)

    def third(h):
        at = cols(h)
        slot = h % 3
        keys2 = jnp.concatenate([rim[:BLOCK, at], k[:, at]], 0)
        values2 = jnp.concatenate([rim[BLOCK:, at], v[:, at]], 0)
        dv, o = spread(p_buf, slot, g[:, at], values2, sv[slot], tri, low)
        dk, dq = spread(ds_buf, slot, sc[slot], keys2, sk[slot], tri, low)
        att[:, at] = o.astype(bf16)
        gq[:, at] = (dq * gain[:, at]).astype(bf16)
        gain_part[:, at] = jnp.sum(dq * q[:, at].astype(f32), 0, keepdims=True)
        out[:BLOCK, at] = dk[:BLOCK].astype(bf16)
        out[BLOCK:, at] = dv[:BLOCK].astype(bf16)
        heads_part[:BLOCK, at] = dk[BLOCK : 2 * BLOCK]
        heads_part[BLOCK:, at] = dv[BLOCK : 2 * BLOCK]
        sum_part[:, :own, at] = dk[2 * BLOCK :].reshape(sources, own, HD)
        sum_part[:, own:, at] = dv[2 * BLOCK :].reshape(sources, own, HD)

    pipeline(H, first, second, third)


def main_kernel(
    segs, rank_ref, q, k, v, g, sums, gain, att_in, gq_in, heads_part, sum_part, gain_in,
    att, gq, gk, gv, tails, payload,
    s_buf, d_buf, p_buf, ds_buf, sc, sk, sv, dk_acc, dv_acc, sum_dk, sum_dv, gain_part, bias_ref,
):
    rank = rank_ref[0]
    sources, both, _ = sums.shape
    own = both // 2
    total_sums = sources * own
    blocks = q.shape[0] // BLOCK
    per_seg = STRIDE // BLOCK

    @pl.when(pl.program_id(0) == 0)
    def _():
        for seg in range(segs):
            bias_ref[2 * seg] = sum_bias(total_sums, rank * segs + seg, True)
            bias_ref[2 * seg + 1] = sum_bias(total_sums, rank * segs + seg, False)

    tri, low = triangle()
    gain_row = gain[...]
    sk[...], sv[...] = unpack_sums(sums)
    att[:BLOCK] = att_in[...]
    gq[:BLOCK] = gq_in[...]
    gain_part[...] = gain_in[...]
    sum_dk[...] = sum_part[:, :own].reshape(total_sums, HD)
    sum_dv[...] = sum_part[:, own:].reshape(total_sums, HD)

    def first(i):
        b = i + 1
        rows = slice(b * BLOCK, (b + 1) * BLOCK)
        two = slice((b - 1) * BLOCK, (b + 1) * BLOCK)
        slot = i % 3
        sc[slot] = (q[rows].astype(f32) * gain_row).astype(bf16)
        score(slot, s_buf, d_buf, k[two], v[two], sk[...], sv[...], sc[slot], g[rows], tri, None)

    def second(i):
        b = i + 1
        bias = bias_ref[2 * (b // per_seg) + (0 if b % per_seg == 0 else 1)]
        soften(i % 3, s_buf, d_buf, p_buf, ds_buf, bias)

    def third(i):
        b = i + 1
        slot = i % 3
        rows = slice(b * BLOCK, (b + 1) * BLOCK)
        before = slice((b - 1) * BLOCK, b * BLOCK)
        two = slice((b - 1) * BLOCK, (b + 1) * BLOCK)
        dv, o = spread(p_buf, slot, g[rows], v[two], sv[...], tri, low)
        dk, dq = spread(ds_buf, slot, sc[slot], k[two], sk[...], tri, low)
        att[rows] = o.astype(bf16)
        gq[rows] = (dq * gain_row).astype(bf16)
        gain_part[...] += jnp.sum(dq * q[rows].astype(f32), 0, keepdims=True)
        sum_dk[...] += dk[2 * BLOCK :]
        sum_dv[...] += dv[2 * BLOCK :]
        if b == 1:
            gk[before] = (heads_part[:BLOCK] + dk[:BLOCK]).astype(bf16)
            gv[before] = (heads_part[BLOCK:] + dv[:BLOCK]).astype(bf16)
        elif b % per_seg == 0:
            at = (b // per_seg - 1) * 2 * BLOCK
            tails[at : at + BLOCK] = dk_acc[...] + dk[:BLOCK]
            tails[at + BLOCK : at + 2 * BLOCK] = dv_acc[...] + dv[:BLOCK]
        else:
            gk[before] = (dk_acc[...] + dk[:BLOCK]).astype(bf16)
            gv[before] = (dv_acc[...] + dv[:BLOCK]).astype(bf16)
        if b == blocks - 1:
            at = (segs - 1) * 2 * BLOCK
            tails[at : at + BLOCK] = dk[BLOCK : 2 * BLOCK]
            tails[at + BLOCK : at + 2 * BLOCK] = dv[BLOCK : 2 * BLOCK]
        else:
            dk_acc[...] = dk[BLOCK : 2 * BLOCK]
            dv_acc[...] = dv[BLOCK : 2 * BLOCK]

    pipeline(blocks - 1, first, second, third)
    payload[:, :both] = jnp.concatenate(
        [sum_dk[...].reshape(sources, own, HD), sum_dv[...].reshape(sources, own, HD)], 1
    ).astype(bf16)
    part = gain_part[...]
    high = part.astype(bf16)
    rest = (part - high.astype(f32)).astype(bf16)
    payload[:, both : both + 1] = jnp.broadcast_to(high[None], (sources, 1, HD))
    payload[:, both + 1 :] = jnp.broadcast_to(rest[None], (sources, 1, HD))


def finish_kernel(segs, gk_in, gv_in, tails, rim, sums, gk, gv):
    del gk_in, gv_in
    seg = pl.program_id(0)
    last = seg == segs - 1
    dk = tails[:BLOCK]
    dv = tails[BLOCK:]
    rim_dk = rim[:BLOCK].astype(f32)
    rim_dv = rim[BLOCK:].astype(f32)
    if segs > 1:
        rim_dk = jnp.where(last, rim_dk, 0.0)
        rim_dv = jnp.where(last, rim_dv, 0.0)
    total = jnp.sum(sums[...].astype(f32), 0)
    own = segs * SUMMARY
    body = BLOCK - SUMMARY
    dk = dk + rim_dk
    dv = dv + rim_dv
    sk = total[:SUMMARY]
    sv = total[own : own + SUMMARY]
    for other in range(1, segs):
        at = other * SUMMARY
        sk = jnp.where(seg == other, total[at : at + SUMMARY], sk)
        sv = jnp.where(seg == other, total[own + at : own + at + SUMMARY], sv)
    gk[...] = jnp.concatenate([dk[:body], dk[body:] + sk], 0).astype(bf16)
    gv[...] = jnp.concatenate([dv[:body], dv[body:] + sv], 0).astype(bf16)


def per_device(queries, keys, values, cotangent, gain):
    batch, length, width = queries.shape
    segs = length // STRIDE
    own = segs * SUMMARY
    n = lax.axis_size("ctx")
    rank = lax.axis_index("ctx")
    total_sums = n * own
    q, k, v, g = (a.reshape(length, width) for a in (queries, keys, values, cotangent))
    gain_row = gain.reshape(1, width)
    rank1 = rank.reshape(1).astype(jnp.int32)

    rim = from_behind(
        jnp.concatenate([k[length - BLOCK :], v[length - BLOCK :]], 0), "ctx", 1
    )
    own_keys = k.reshape(segs, STRIDE, width)[:, STRIDE - SUMMARY :].reshape(own, width)
    own_values = v.reshape(segs, STRIDE, width)[:, STRIDE - SUMMARY :].reshape(own, width)
    own_both = jnp.concatenate([own_keys, own_values], 0)
    sums = lax.all_to_all(jnp.broadcast_to(own_both[None], (n, 2 * own, width)), "ctx", 0, 0)

    smem = pl.BlockSpec(memory_space=pltpu.SMEM)
    whole = lambda *shape: pl.BlockSpec(shape, lambda i: (0,) * len(shape))
    raw = pl.BlockSpec(memory_space=pl.ANY)
    col = lambda rows: pl.BlockSpec((rows, HD), lambda h: (0, h))
    col3 = pl.BlockSpec((n, 2 * own, HD), lambda h: (0, 0, h))
    big = jax.ShapeDtypeStruct((length, width), bf16)
    wide = BLOCK + total_sums
    buffers = [
        pltpu.VMEM((3, wide, BLOCK), f32),
        pltpu.VMEM((3, wide, BLOCK), f32),
        pltpu.VMEM((3, wide, BLOCK), bf16),
        pltpu.VMEM((3, wide, BLOCK), bf16),
        pltpu.VMEM((3, BLOCK, HD), bf16),
    ]
    first = whole(BLOCK, width)
    part3 = whole(n, 2 * own, width)
    small = [
        jax.ShapeDtypeStruct((BLOCK, width), bf16),
        jax.ShapeDtypeStruct((BLOCK, width), bf16),
        jax.ShapeDtypeStruct((2 * BLOCK, width), bf16),
        jax.ShapeDtypeStruct((2 * BLOCK, width), f32),
        jax.ShapeDtypeStruct((n, 2 * own, width), f32),
        jax.ShapeDtypeStruct((1, width), f32),
    ]
    rim_call = pl.pallas_call(
        functools.partial(rim_kernel, segs),
        grid=(1,),
        in_specs=[smem] + [first] * 4 + [whole(2 * BLOCK, width), part3, whole(1, width)],
        out_specs=[first] * 2 + [whole(2 * BLOCK, width)] * 2 + [part3, whole(1, width)],
        out_shape=small,
        scratch_shapes=buffers + [
            pltpu.VMEM((3, total_sums, HD), bf16),
            pltpu.VMEM((3, total_sums, HD), bf16),
        ],
        cost_estimate=pl.CostEstimate(flops=500_000_000, bytes_accessed=5 << 20, transcendentals=0),
        name="rim_grads",
    )
    att0, gq0, rim_grads, heads_part, sum_part, gain_part = rim_call(
        rank1, q, k, v, g, rim, sums, gain_row
    )
    received = from_behind(rim_grads, "ctx", -1)

    near = pl.BlockSpec((BLOCK, HD), lambda h: (0, h))
    col3_gain = pl.BlockSpec((n, 2 * own + 2, HD), lambda h: (0, 0, h))
    main = pl.pallas_call(
        functools.partial(main_kernel, segs),
        grid=(H,),
        in_specs=[smem] + [col(length)] * 4 + [col3, col(1), near, near, col(2 * BLOCK), col3,
                  col(1)],
        out_specs=[col(length)] * 4 + [col(segs * 2 * BLOCK), col3_gain],
        out_shape=[big] * 4 + [
            jax.ShapeDtypeStruct((segs * 2 * BLOCK, width), f32),
            jax.ShapeDtypeStruct((n, 2 * own + 2, width), bf16),
        ],
        scratch_shapes=buffers + [
            pltpu.VMEM((total_sums, HD), bf16),
            pltpu.VMEM((total_sums, HD), bf16),
            pltpu.VMEM((BLOCK, HD), f32),
            pltpu.VMEM((BLOCK, HD), f32),
            pltpu.VMEM((total_sums, HD), f32),
            pltpu.VMEM((total_sums, HD), f32),
            pltpu.VMEM((1, HD), f32),
            pltpu.VMEM((2 * segs, total_sums, BLOCK), f32),
        ],
        cost_estimate=pl.CostEstimate(
            flops=4_000_000_000, bytes_accessed=18 << 20, transcendentals=2_000_000
        ),
        name="band_and_sums",
    )
    att, gq, gk, gv, tails, payload = main(
        rank1, q, k, v, g, sums, gain_row, att0, gq0, heads_part, sum_part, gain_part
    )

    got = lax.all_to_all(payload, "ctx", 0, 0)
    gain_total = jnp.sum(got[:, 2 * own :].astype(f32), (0, 1))
    rows = lax.axis_size("dp")
    step = 1
    while step < rows:
        other = lax.ppermute(gain_total, "dp", [(i, i ^ step) for i in range(rows)])
        gain_total = gain_total + other
        step *= 2
    gain_grad = gain_total * (batch * length * n * rows) ** -0.5

    per_seg = STRIDE // BLOCK
    tail_spec = pl.BlockSpec((2 * BLOCK, width), lambda s: (s, 0))
    last_block = pl.BlockSpec((BLOCK, width), lambda s: (s * per_seg + per_seg - 1, 0))
    finish = pl.pallas_call(
        functools.partial(finish_kernel, segs),
        grid=(segs,),
        in_specs=[raw, raw, tail_spec, whole(2 * BLOCK, width), whole(n, 2 * own + 2, width)],
        out_specs=[last_block, last_block],
        out_shape=[big, big],
        input_output_aliases={0: 0, 1: 1},
        cost_estimate=pl.CostEstimate(flops=1_000_000, bytes_accessed=3 << 20, transcendentals=0),
        name="finish",
    )
    gk, gv = finish(gk, gv, tails, received, got)
    return (
        att.reshape(queries.shape), gq.reshape(queries.shape), gk.reshape(queries.shape),
        gv.reshape(queries.shape), gain_grad,
    )


def solution(mesh):
    spec = P("dp", "ctx", None)
    return jax.shard_map(
        per_device, mesh=mesh, in_specs=(spec,) * 4 + (P(),), out_specs=(spec,) * 4 + (P(),),
        check_vma=False,
    )
```

```python
import functools

import jax
import jax.numpy as jnp
from jax import lax
from jax.experimental import pallas as pl
from jax.experimental.pallas import tpu as pltpu
from jax.sharding import PartitionSpec as P


H = 8
HD = 128
BLOCK = 128
STRIDE = 1024
SUMMARY = 8
NEG = -1e30
SCALE = HD**-0.5
EXP2_SCALE = SCALE * 1.4426950408889634

f32 = jnp.float32
bf16 = jnp.bfloat16


def from_behind(value, axis, steps):
    count = lax.axis_size(axis)
    first, last = (max(0, -steps), min(count, count - steps))
    return lax.ppermute(value, axis, [(source, source + steps) for source in range(first, last)])


def nt(a, b):
    return lax.dot_general(a, b, (((1,), (1,)), ((), ())), preferred_element_type=f32)


def nn(a, b):
    return lax.dot_general(a, b, (((1,), (0,)), ((), ())), preferred_element_type=f32)


def unpack_sums(ref):
    wide = ref[...].astype(f32)
    sources, both, width = wide.shape
    own = both // 2
    keys = wide[:, :own].reshape(sources * own, width)
    values = wide[:, own:].reshape(sources * own, width)
    return keys.astype(bf16), values.astype(bf16)


def sum_bias(total_sums, segment, first_block):
    slot = lax.broadcasted_iota(jnp.int32, (total_sums, BLOCK), 0)
    query = lax.broadcasted_iota(jnp.int32, (total_sums, BLOCK), 1)
    position = slot // SUMMARY * STRIDE + STRIDE - SUMMARY + slot % SUMMARY
    start = segment * STRIDE + (0 if first_block else BLOCK)
    return jnp.where(start + query - position >= BLOCK, 0.0, NEG).astype(f32)


def pipeline(count, first, second, third):
    for step in range(count + 2):
        if step < count:
            first(step)
        if 0 <= step - 2:
            third(step - 2)
        if 0 <= step - 1 < count:
            second(step - 1)


def triangle():
    at = [lax.broadcasted_iota(jnp.int32, (BLOCK, BLOCK), axis) for axis in (0, 1)]
    return at[0] <= at[1], at[1] <= at[0]


def score(slot, s_buf, d_buf, keys2, values2, sum_keys, sum_values, scaled, grads, tri, no_prev):
    s = nt(keys2, scaled)
    prev = s[:BLOCK]
    if no_prev is not None:
        prev = jnp.where(no_prev, NEG, prev)
    s_buf[slot, :BLOCK] = jnp.where(tri, s[BLOCK:], prev)
    s_buf[slot, BLOCK:] = nt(sum_keys, scaled)
    d = nt(values2, grads)
    d_buf[slot, :BLOCK] = jnp.where(tri, d[BLOCK:], d[:BLOCK])
    d_buf[slot, BLOCK:] = nt(sum_values, grads)


def soften(slot, s_buf, d_buf, p_out, ds_out, dss_out, bias):
    sm = s_buf[slot, :BLOCK]
    ss = s_buf[slot, BLOCK:] + bias
    top = jnp.maximum(jnp.max(sm, 0, keepdims=True), jnp.max(ss, 0, keepdims=True))
    e = jnp.exp2((sm - top) * EXP2_SCALE)
    es = jnp.exp2((ss - top) * EXP2_SCALE)
    total = jnp.sum(e, 0, keepdims=True) + jnp.sum(es, 0, keepdims=True)
    inv = 1.0 / total
    p = e * inv
    ps = es * inv
    p_out[:BLOCK] = p.astype(bf16)
    p_out[BLOCK:] = ps.astype(bf16)
    dm = d_buf[slot, :BLOCK]
    dsum = d_buf[slot, BLOCK:]
    delta = jnp.sum(p * dm, 0, keepdims=True) + jnp.sum(ps * dsum, 0, keepdims=True)
    ds_out[...] = (p * (dm - delta) * SCALE).astype(bf16)
    dss_out[...] = (ps * (dsum - delta) * SCALE).astype(bf16)


def spread(buf, slot, rhs_by_query, rhs_by_key, rhs_by_sum, tri, low):
    zero = jnp.zeros((BLOCK, BLOCK), bf16)
    m = buf[slot, :BLOCK]
    ms = buf[slot, BLOCK:]
    by_key = nn(
        jnp.concatenate([jnp.where(tri, zero, m), jnp.where(tri, m, zero), ms], 0), rhs_by_query
    )
    mt = m.T
    wide = jnp.concatenate([jnp.where(low, zero, mt), jnp.where(low, mt, zero)], 1)
    by_query = nn(wide, rhs_by_key) + nn(ms.T, rhs_by_sum)
    return by_key, by_query


def rim_kernel(
    segs, rank_ref, q, k, v, g, rim, sums, gain,
    att, gq, out, heads_part, sum_part, gain_part,
    s_buf, d_buf, p_buf, ds_buf, sc, sk, sv,
):
    rank = rank_ref[0]
    sources, both, _ = sums.shape
    own = both // 2
    total_sums = sources * own
    bias = sum_bias(total_sums, rank * segs, True)
    tri, low = triangle()

    def cols(h):
        return slice(h * HD, (h + 1) * HD)

    def first(h):
        at = cols(h)
        slot = h % 3
        sk[slot], sv[slot] = unpack_sums(sums.at[:, :, at])
        sc[slot] = (q[:, at].astype(f32) * gain[:, at]).astype(bf16)
        keys2 = jnp.concatenate([rim[:BLOCK, at], k[:, at]], 0)
        values2 = jnp.concatenate([rim[BLOCK:, at], v[:, at]], 0)
        score(slot, s_buf, d_buf, keys2, values2, sk[slot], sv[slot], sc[slot], g[:, at], tri,
              rank == 0)

    def second(h):
        ds = ds_buf.at[h % 3]
        soften(h % 3, s_buf, d_buf, p_buf.at[h % 3], ds.at[:BLOCK], ds.at[BLOCK:], bias)

    def third(h):
        at = cols(h)
        slot = h % 3
        keys2 = jnp.concatenate([rim[:BLOCK, at], k[:, at]], 0)
        values2 = jnp.concatenate([rim[BLOCK:, at], v[:, at]], 0)
        dv, o = spread(p_buf, slot, g[:, at], values2, sv[slot], tri, low)
        dk, dq = spread(ds_buf, slot, sc[slot], keys2, sk[slot], tri, low)
        att[:, at] = o.astype(bf16)
        gq[:, at] = (dq * gain[:, at]).astype(bf16)
        gain_part[:, at] = jnp.sum(dq * q[:, at].astype(f32), 0, keepdims=True)
        out[:BLOCK, at] = dk[:BLOCK].astype(bf16)
        out[BLOCK:, at] = dv[:BLOCK].astype(bf16)
        heads_part[:BLOCK, at] = dk[BLOCK : 2 * BLOCK]
        heads_part[BLOCK:, at] = dv[BLOCK : 2 * BLOCK]
        sum_part[:, :own, at] = dk[2 * BLOCK :].reshape(sources, own, HD)
        sum_part[:, own:, at] = dv[2 * BLOCK :].reshape(sources, own, HD)

    pipeline(H, first, second, third)


def main_kernel(
    segs, rank_ref, q, k, v, g, sums, gain, gq_in, sum_part, gain_in,
    gq, p_out, ds_out, payload,
    s_buf, d_buf, dss_buf, sc, sk, sv, sum_dk, sum_dv, gain_part, bias_ref,
):
    rank = rank_ref[0]
    sources, both, _ = sums.shape
    own = both // 2
    total_sums = sources * own
    wide = BLOCK + total_sums
    blocks = q.shape[0] // BLOCK
    per_seg = STRIDE // BLOCK

    @pl.when(pl.program_id(0) == 0)
    def _():
        for seg in range(segs):
            bias_ref[2 * seg] = sum_bias(total_sums, rank * segs + seg, True)
            bias_ref[2 * seg + 1] = sum_bias(total_sums, rank * segs + seg, False)

    tri, low = triangle()
    zero = jnp.zeros((BLOCK, BLOCK), bf16)
    gain_row = gain[...]
    sk[...], sv[...] = unpack_sums(sums)
    gq[:BLOCK] = gq_in[...]
    gain_part[...] = gain_in[...]
    sum_dk[...] = sum_part[:, :own].reshape(total_sums, HD)
    sum_dv[...] = sum_part[:, own:].reshape(total_sums, HD)

    def first(i):
        b = i + 1
        slot = i % 3
        rows = slice(b * BLOCK, (b + 1) * BLOCK)
        two = slice((b - 1) * BLOCK, (b + 1) * BLOCK)
        sc[slot] = (q[rows].astype(f32) * gain_row).astype(bf16)
        score(slot, s_buf, d_buf, k[two], v[two], sk[...], sv[...], sc[slot], g[rows], tri, None)

    def second(i):
        b = i + 1
        bias = bias_ref[2 * (b // per_seg) + (0 if b % per_seg == 0 else 1)]
        at = i * wide
        soften(
            i % 3, s_buf, d_buf, p_out.at[at : at + wide], ds_out.at[i * BLOCK : b * BLOCK],
            dss_buf.at[i % 3], bias,
        )

    def third(i):
        b = i + 1
        slot = i % 3
        rows = slice(b * BLOCK, (b + 1) * BLOCK)
        two = slice((b - 1) * BLOCK, (b + 1) * BLOCK)
        ms = dss_buf[slot]
        mt = ds_out[i * BLOCK : b * BLOCK].T
        pair = jnp.concatenate([jnp.where(low, zero, mt), jnp.where(low, mt, zero)], 1)
        dq = nn(pair, k[two]) + nn(ms.T, sk[...])
        gq[rows] = (dq * gain_row).astype(bf16)
        gain_part[...] += jnp.sum(dq * q[rows].astype(f32), 0, keepdims=True)
        sum_dk[...] += nn(ms, sc[slot])
        sum_dv[...] += nn(p_out[i * wide + BLOCK : (i + 1) * wide], g[rows])

    pipeline(blocks - 1, first, second, third)
    payload[:, :both] = jnp.concatenate(
        [sum_dk[...].reshape(sources, own, HD), sum_dv[...].reshape(sources, own, HD)], 1
    ).astype(bf16)
    part = gain_part[...]
    high = part.astype(bf16)
    rest = (part - high.astype(f32)).astype(bf16)
    payload[:, both : both + 1] = jnp.broadcast_to(high[None], (sources, 1, HD))
    payload[:, both + 1 :] = jnp.broadcast_to(rest[None], (sources, 1, HD))


def own_kernel(q, v, g, p_in, ds_in, sums, gain, att_in, heads_part, att, gk, gv, tails, sc):
    for h in range(q.shape[1] // HD):
        at = slice(h * HD, (h + 1) * HD)
        heads = q.shape[1] // HD
        p_rows = p_in.shape[0] // heads
        ds_rows = ds_in.shape[0] // heads
        own_head(
            q.at[:, at], v.at[:, at], g.at[:, at],
            p_in.at[h * p_rows : (h + 1) * p_rows], ds_in.at[h * ds_rows : (h + 1) * ds_rows],
            sums.at[:, :, at], gain.at[:, at], att_in.at[:, at], heads_part.at[:, at],
            att.at[:, at], gk.at[:, at], gv.at[:, at], tails.at[:, at], sc.at[h],
        )


def own_head(q, v, g, p_in, ds_in, sums, gain, att_in, heads_part, att, gk, gv, tails, sc):
    blocks = q.shape[0] // BLOCK
    per_seg = STRIDE // BLOCK
    _, sv = unpack_sums(sums)
    wide = BLOCK + sv.shape[0]
    tri, low = triangle()
    zero = jnp.zeros((BLOCK, BLOCK), bf16)
    sc[...] = (q[...].astype(f32) * gain[...]).astype(bf16)
    att[:BLOCK] = att_in[...]
    for b in range(blocks):
        rows = slice(b * BLOCK, (b + 1) * BLOCK)
        if b > 0:
            at = (b - 1) * wide
            p = p_in[at : at + BLOCK]
            pt = p.T
            pair = jnp.concatenate([jnp.where(low, zero, pt), jnp.where(low, pt, zero)], 1)
            o = nn(pair, v[(b - 1) * BLOCK : (b + 1) * BLOCK])
            att[rows] = (o + nn(p_in[at + BLOCK : at + wide].T, sv)).astype(bf16)
            p_own = jnp.where(tri, p, zero)
            ds_own = jnp.where(tri, ds_in[(b - 1) * BLOCK : rows.start], zero)
        if b < blocks - 1:
            p_next = jnp.where(tri, zero, p_in[b * wide : b * wide + BLOCK])
            ds_next = jnp.where(tri, zero, ds_in[b * BLOCK : (b + 1) * BLOCK])
        if b == 0:
            following = slice(BLOCK, 2 * BLOCK)
            dk = heads_part[:BLOCK] + nn(ds_next, sc[following])
            dv = heads_part[BLOCK:] + nn(p_next, g[following])
        elif b < blocks - 1:
            both = slice(b * BLOCK, (b + 2) * BLOCK)
            dk = nn(jnp.concatenate([ds_own, ds_next], 1), sc[both])
            dv = nn(jnp.concatenate([p_own, p_next], 1), g[both])
        else:
            dk = nn(ds_own, sc[rows])
            dv = nn(p_own, g[rows])
        if b % per_seg == per_seg - 1:
            at = b // per_seg * 2 * BLOCK
            tails[at : at + BLOCK] = dk
            tails[at + BLOCK : at + 2 * BLOCK] = dv
        else:
            gk[rows] = dk.astype(bf16)
            gv[rows] = dv.astype(bf16)


def finish_kernel(segs, gk_in, gv_in, tails, rim, sums, gk, gv):
    del gk_in, gv_in
    seg = pl.program_id(0)
    last = seg == segs - 1
    dk = tails[:BLOCK]
    dv = tails[BLOCK:]
    rim_dk = rim[:BLOCK].astype(f32)
    rim_dv = rim[BLOCK:].astype(f32)
    if segs > 1:
        rim_dk = jnp.where(last, rim_dk, 0.0)
        rim_dv = jnp.where(last, rim_dv, 0.0)
    total = jnp.sum(sums[...].astype(f32), 0)
    own = segs * SUMMARY
    body = BLOCK - SUMMARY
    dk = dk + rim_dk
    dv = dv + rim_dv
    sk = total[:SUMMARY]
    sv = total[own : own + SUMMARY]
    for other in range(1, segs):
        at = other * SUMMARY
        sk = jnp.where(seg == other, total[at : at + SUMMARY], sk)
        sv = jnp.where(seg == other, total[own + at : own + at + SUMMARY], sv)
    gk[...] = jnp.concatenate([dk[:body], dk[body:] + sk], 0).astype(bf16)
    gv[...] = jnp.concatenate([dv[:body], dv[body:] + sv], 0).astype(bf16)


def per_device(queries, keys, values, cotangent, gain):
    batch, length, width = queries.shape
    segs = length // STRIDE
    own = segs * SUMMARY
    n = lax.axis_size("ctx")
    rank = lax.axis_index("ctx")
    total_sums = n * own
    q, k, v, g = (a.reshape(length, width) for a in (queries, keys, values, cotangent))
    gain_row = gain.reshape(1, width)
    rank1 = rank.reshape(1).astype(jnp.int32)

    rim = from_behind(
        jnp.concatenate([k[length - BLOCK :], v[length - BLOCK :]], 0), "ctx", 1
    )
    own_keys = k.reshape(segs, STRIDE, width)[:, STRIDE - SUMMARY :].reshape(own, width)
    own_values = v.reshape(segs, STRIDE, width)[:, STRIDE - SUMMARY :].reshape(own, width)
    own_both = jnp.concatenate([own_keys, own_values], 0)
    sums = lax.all_to_all(jnp.broadcast_to(own_both[None], (n, 2 * own, width)), "ctx", 0, 0)

    smem = pl.BlockSpec(memory_space=pltpu.SMEM)
    whole = lambda *shape: pl.BlockSpec(shape, lambda i: (0,) * len(shape))
    raw = pl.BlockSpec(memory_space=pl.ANY)
    col = lambda rows: pl.BlockSpec((rows, HD), lambda h: (0, h))
    col3 = pl.BlockSpec((n, 2 * own, HD), lambda h: (0, 0, h))
    big = jax.ShapeDtypeStruct((length, width), bf16)
    wide = BLOCK + total_sums
    buffers = [
        pltpu.VMEM((3, wide, BLOCK), f32),
        pltpu.VMEM((3, wide, BLOCK), f32),
        pltpu.VMEM((3, wide, BLOCK), bf16),
        pltpu.VMEM((3, wide, BLOCK), bf16),
        pltpu.VMEM((3, BLOCK, HD), bf16),
    ]
    first = whole(BLOCK, width)
    part3 = whole(n, 2 * own, width)
    small = [
        jax.ShapeDtypeStruct((BLOCK, width), bf16),
        jax.ShapeDtypeStruct((BLOCK, width), bf16),
        jax.ShapeDtypeStruct((2 * BLOCK, width), bf16),
        jax.ShapeDtypeStruct((2 * BLOCK, width), f32),
        jax.ShapeDtypeStruct((n, 2 * own, width), f32),
        jax.ShapeDtypeStruct((1, width), f32),
    ]
    rim_call = pl.pallas_call(
        functools.partial(rim_kernel, segs),
        grid=(1,),
        in_specs=[smem] + [first] * 4 + [whole(2 * BLOCK, width), part3, whole(1, width)],
        out_specs=[first] * 2 + [whole(2 * BLOCK, width)] * 2 + [part3, whole(1, width)],
        out_shape=small,
        scratch_shapes=buffers + [
            pltpu.VMEM((3, total_sums, HD), bf16),
            pltpu.VMEM((3, total_sums, HD), bf16),
        ],
        cost_estimate=pl.CostEstimate(flops=500_000_000, bytes_accessed=5 << 20, transcendentals=0),
        name="rim_grads",
    )
    att0, gq0, rim_grads, heads_part, sum_part, gain_part = rim_call(
        rank1, q, k, v, g, rim, sums, gain_row
    )
    received = from_behind(rim_grads, "ctx", -1)

    near = pl.BlockSpec((BLOCK, HD), lambda h: (0, h))
    col3_gain = pl.BlockSpec((n, 2 * own + 2, HD), lambda h: (0, 0, h))
    packed = lambda rows: pl.BlockSpec((rows, HD), lambda h: (h, 0))
    later = length // BLOCK - 1
    main = pl.pallas_call(
        functools.partial(main_kernel, segs),
        grid=(H,),
        in_specs=[smem] + [col(length)] * 4 + [col3, col(1), near, col3, col(1)],
        out_specs=[col(length), packed(later * wide), packed(later * BLOCK), col3_gain],
        out_shape=[
            big,
            jax.ShapeDtypeStruct((H * later * wide, HD), bf16),
            jax.ShapeDtypeStruct((H * later * BLOCK, HD), bf16),
            jax.ShapeDtypeStruct((n, 2 * own + 2, width), bf16),
        ],
        scratch_shapes=[
            pltpu.VMEM((3, wide, BLOCK), f32),
            pltpu.VMEM((3, wide, BLOCK), f32),
            pltpu.VMEM((3, total_sums, BLOCK), bf16),
            pltpu.VMEM((3, BLOCK, HD), bf16),
            pltpu.VMEM((total_sums, HD), bf16),
            pltpu.VMEM((total_sums, HD), bf16),
            pltpu.VMEM((total_sums, HD), f32),
            pltpu.VMEM((total_sums, HD), f32),
            pltpu.VMEM((1, HD), f32),
            pltpu.VMEM((2 * segs, total_sums, BLOCK), f32),
        ],
        cost_estimate=pl.CostEstimate(
            flops=2_500_000_000, bytes_accessed=16 << 20, transcendentals=2_000_000
        ),
        name="soft",
    )
    gq, p_all, ds_all, payload = main(rank1, q, k, v, g, sums, gain_row, gq0, sum_part, gain_part)

    group = 2
    slab = lambda rows: pl.BlockSpec((rows, group * HD), lambda h: (0, h))
    slab3 = pl.BlockSpec((n, 2 * own, group * HD), lambda h: (0, 0, h))
    ours = pl.pallas_call(
        own_kernel,
        grid=(H // group,),
        in_specs=[slab(length)] * 3 + [packed(group * later * wide), packed(group * later * BLOCK),
                  slab3, slab(1), slab(BLOCK), slab(2 * BLOCK)],
        out_specs=[slab(length)] * 3 + [slab(segs * 2 * BLOCK)],
        out_shape=[big] * 3 + [jax.ShapeDtypeStruct((segs * 2 * BLOCK, width), f32)],
        scratch_shapes=[pltpu.VMEM((group, length, HD), bf16)],
        cost_estimate=pl.CostEstimate(
            flops=1_500_000_000, bytes_accessed=20 << 20, transcendentals=0
        ),
        name="own_grads",
    )
    att, gk, gv, tails = ours(q, v, g, p_all, ds_all, sums, gain_row, att0, heads_part)

    got = lax.all_to_all(payload, "ctx", 0, 0)
    gain_total = jnp.sum(got[:, 2 * own :].astype(f32), (0, 1))
    rows = lax.axis_size("dp")
    step = 1
    while step < rows:
        other = lax.ppermute(gain_total, "dp", [(i, i ^ step) for i in range(rows)])
        gain_total = gain_total + other
        step *= 2
    gain_grad = gain_total * (batch * length * n * rows) ** -0.5

    per_seg = STRIDE // BLOCK
    tail_spec = pl.BlockSpec((2 * BLOCK, width), lambda s: (s, 0))
    last_block = pl.BlockSpec((BLOCK, width), lambda s: (s * per_seg + per_seg - 1, 0))
    finish = pl.pallas_call(
        functools.partial(finish_kernel, segs),
        grid=(segs,),
        in_specs=[raw, raw, tail_spec, whole(2 * BLOCK, width), whole(n, 2 * own + 2, width)],
        out_specs=[last_block, last_block],
        out_shape=[big, big],
        input_output_aliases={0: 0, 1: 1},
        cost_estimate=pl.CostEstimate(flops=1_000_000, bytes_accessed=3 << 20, transcendentals=0),
        name="finish",
    )
    gk, gv = finish(gk, gv, tails, received, got)
    return (
        att.reshape(queries.shape), gq.reshape(queries.shape), gk.reshape(queries.shape),
        gv.reshape(queries.shape), gain_grad,
    )


def solution(mesh):
    spec = P("dp", "ctx", None)
    return jax.shard_map(
        per_device, mesh=mesh, in_specs=(spec,) * 4 + (P(),), out_specs=(spec,) * 4 + (P(),),
        check_vma=False,
    )
```
